32 devices in a mesh: groups: 2 (over y), row: 4 (over z), col: 4 (over x, core).
Axes of the slice: x: 2, y: 2, z: 4, core: 2. Of those that a mesh axis runs over, the one named last changes fastest.
Arguments:
- alignment: bfloat16 [256, 128, 256], P(('groups', 'row'), 'col'), parts along dimension 0, may hold values from -6 to 6
- sequence_mask: int32 [256], P('groups'), parts along dimension 0, may hold values 0 or 1
- residue_mask: int32 [256], P('groups'), parts along dimension 0, may hold values 0 or 1
- layer_norm_gain: float32 [256], replicated, may hold values from 0.5 to 1.5
- norm_shift: float32 [256], replicated, may hold values from -3 to 3
- proj_weight: bfloat16 [256, 64], replicated, may hold values from -0.375 to 0.375
- proj_bias: float32 [64], replicated, may hold values from -3 to 3
- out_weight: bfloat16 [1024, 128], replicated, may hold values from -2 to 2
- out_bias: float32 [128], replicated, may hold values from -4 to 4
- cotangent: bfloat16 [256, 128, 128], P(('groups', 'row'), 'col'), parts along dimension 0, may hold values from -2 to 2
Outputs:
- pair_output_update: bfloat16 [256, 128, 128], P(('groups', 'row'), 'col'), parts along dimension 0
- alignment_gradient: bfloat16 [256, 128, 256], P(('groups', 'row'), 'col'), parts along dimension 0
- norm_gain_gradient: float32 [512], P('groups'), parts along dimension 0
- norm_shift_gradient: float32 [512], P('groups'), parts along dimension 0
- projection_weight_gradient: float32 [512, 64], P('groups'), parts along dimension 0
- projection_bias_gradient: float32 [128], P('groups'), parts along dimension 0
- output_weight_gradient: float32 [2048, 128], P('groups'), parts along dimension 0
The draws below stay inside these ranges and needn't reach their ends.
There are 2 independent parts, one for each index of `groups`. The reference program is written for one: setup_inputs(seed, part) draws one part's arguments, and reference() takes and returns one part's arrays. A program takes and returns all parts, laid end to end along the dimension named above; an argument that names none is the same for every part. Nothing has to cross between parts.
All inputs are finite; a program needn't handle non-finite values.
Results may differ from the reference program's by a relative error of at most 0.0074.
Values may be sent and summed in bfloat16 or wider, within the bound.
A program may use at most 64 MiB of HBM per device.

```python
import jax
import jax.numpy as jnp
from jax import lax

C = 256
HID = 32
PAIR = 128
SEQS = 128
N = 128


def with_ends(values, rng, smallest, high):
    place = [jax.random.randint(jax.random.fold_in(rng, axis), (), 0, length) for axis, length in enumerate(values.shape)]
    widest = values.shape.index(max(values.shape))
    next_to = place[:widest] + [(place[widest] + 1) % values.shape[widest]] + place[widest + 1:]
    return values.at[tuple(place)].set(smallest).at[tuple(next_to)].set(high)


def block_levels(stream_key, extent, split, smallest, largest):
    def one(dim, shards_of):
        steps = jax.random.uniform(jax.random.fold_in(jax.random.fold_in(stream_key, 6), dim), (shards_of,), jnp.float32, smallest / len(split), largest / len(split))
        return jnp.repeat(jnp.exp(steps), extent[dim] // shards_of).reshape((-1,) + (1,) * (len(extent) - dim - 1))

    loudness = one(*split[0])
    for cut in split[1:]:
        loudness = loudness * one(*cut)
    return loudness


def bell_draw(own_key, dims, spread, most, shards=(), kind=jnp.bfloat16):
    level = block_levels(own_key, dims, shards, -0.22, 0.18) if shards else 1.0
    entries = jax.random.normal(own_key, dims, jnp.float32) * spread * level
    return jnp.minimum(jnp.maximum(entries, -most), most).astype(kind)


def setup_inputs(seed: int = 0, part: int = 0) -> dict:
    arg_keys = jax.random.split(jax.random.key(seed), 11)
    own_keys = jax.random.split(jax.random.fold_in(arg_keys[10], part), 11)
    return {
        "alignment": bell_draw(own_keys[0], (SEQS, N, C), 1.0, 6.0, ((0, 4), (1, 4))),
        "sequence_mask": with_ends((jax.random.randint(own_keys[1], (SEQS,), 0, 4) < 3).astype(jnp.int32), jax.random.fold_in(own_keys[1], 1), 0, 1),
        "residue_mask": with_ends((jax.random.randint(own_keys[2], (N,), 0, 8) < 7).astype(jnp.int32), jax.random.fold_in(own_keys[2], 1), 0, 1),
        "layer_norm_gain": jnp.clip(1.0 + 0.1 * jax.random.normal(arg_keys[3], (C,), jnp.float32), 0.5, 1.5),
        "norm_shift": bell_draw(arg_keys[4], (C,), 0.5, 3.0, (), jnp.float32),
        "proj_weight": bell_draw(arg_keys[5], (C, 2 * HID), C ** -0.5, 0.375),
        "proj_bias": bell_draw(arg_keys[6], (2 * HID,), 0.5, 3.0, (), jnp.float32),
        "out_weight": bell_draw(arg_keys[7], (HID * HID, PAIR), (max(1, HID * HID // SEQS)) ** -0.5, 2.0),
        "out_bias": bell_draw(arg_keys[8], (PAIR,), 1.0, 4.0, (), jnp.float32),
        "cotangent": bell_draw(own_keys[9], (N, N, PAIR), 0.3, 2.0, ((0, 4), (1, 4))),
    }


EPSILON = 1e-05

def normalize(values, layer_norm_gain, norm_shift):
    widened = values.astype(jnp.float32)
    centred = widened - lax.optimization_barrier(jnp.mean(widened, axis=-1, keepdims=True))
    inverse_deviation = lax.rsqrt(lax.optimization_barrier(jnp.mean(centred * centred, axis=-1, keepdims=True)) + EPSILON)
    scaled_product = centred * inverse_deviation
    return (scaled_product, inverse_deviation, (scaled_product * layer_norm_gain + norm_shift).astype(jnp.bfloat16))

def layer_norm_backward_pass(normalized_input_gradient, scaled_product, inverse_deviation, layer_norm_gain):
    grad_scaled = normalized_input_gradient * layer_norm_gain
    first = lax.optimization_barrier(jnp.mean(grad_scaled, axis=-1, keepdims=True))
    second = lax.optimization_barrier(jnp.mean(grad_scaled * scaled_product, axis=-1, keepdims=True))
    return inverse_deviation * (grad_scaled - first - scaled_product * second)

def outer_block(left_block, right_flat, hidden, width_j):
    product = lax.dot_general(left_block, right_flat, (((0,), (0,)), ((), ())), preferred_element_type=jnp.float32)
    count_i = left_block.shape[1] // hidden
    product = product.reshape(count_i, hidden, width_j, hidden).transpose(0, 2, 1, 3)
    return product.reshape(count_i * width_j, hidden * hidden).astype(jnp.bfloat16)

def outer_adjoint(grad_outer, count_i, width_j, hidden):
    arranged = grad_outer.reshape(count_i, width_j, hidden, hidden).transpose(0, 2, 1, 3)
    return arranged.reshape(count_i * hidden, width_j * hidden)

def reference(alignment, sequence_mask, residue_mask, layer_norm_gain, norm_shift, proj_weight, proj_bias, out_weight, out_bias, cotangent):
    scaled_product, inverse_deviation, normed = normalize(alignment, layer_norm_gain, norm_shift)
    live = (sequence_mask[:, None] * residue_mask[None, :]).astype(jnp.float32)
    projected = jnp.dot(normed.reshape(SEQS * N, C), proj_weight, preferred_element_type=jnp.float32)
    projected = projected.reshape(SEQS, N, 2 * HID) + proj_bias
    masked = (projected * live[:, :, None]).astype(jnp.bfloat16)
    left_flat = masked[:, :, :HID].reshape(SEQS, N * HID)
    right_flat = masked[:, :, HID:].reshape(SEQS, N * HID)
    kept_count = jnp.sum(sequence_mask).astype(jnp.float32)
    residue_live = residue_mask.astype(jnp.float32)
    block_rows = min(N, 64)

    def advance(running, block_index):
        grad_out_w, grad_right = running
        offset = block_index * block_rows
        left_block = lax.dynamic_slice_in_dim(left_flat, offset * HID, block_rows * HID, 1)
        products = outer_block(left_block, right_flat, HID, N)
        preact = jnp.dot(products, out_weight, preferred_element_type=jnp.float32) + out_bias
        live_rows = lax.dynamic_slice_in_dim(residue_live, offset, block_rows)
        divisor = jnp.maximum(kept_count * live_rows[:, None] * residue_live[None, :], 1.0).reshape(-1, 1)
        pair_block = (preact / divisor).astype(jnp.bfloat16)
        cot_block = lax.dynamic_slice_in_dim(cotangent, offset, block_rows, 0).reshape(-1, PAIR).astype(jnp.float32)
        grad_pre = (cot_block / divisor).astype(jnp.bfloat16)
        grad_out_w = grad_out_w + lax.dot_general(products, grad_pre, (((0,), (0,)), ((), ())), preferred_element_type=jnp.float32)
        grad_outer = jnp.dot(grad_pre, out_weight.T, preferred_element_type=jnp.float32).astype(jnp.bfloat16)
        grad_pairs = outer_adjoint(grad_outer, block_rows, N, HID)
        grad_left = lax.dot_general(right_flat, grad_pairs, (((1,), (1,)), ((), ())), preferred_element_type=jnp.float32)
        grad_right = grad_right + jnp.dot(left_block, grad_pairs, preferred_element_type=jnp.float32)
        return ((grad_out_w, grad_right), (pair_block, grad_left))
    initial = (jnp.zeros((HID * HID, PAIR), jnp.float32), jnp.zeros((SEQS, N * HID), jnp.float32))
    (output_weight_gradient, grad_right), (pair_blocks, grad_lefts) = lax.scan(advance, initial, jnp.arange(N // block_rows, dtype=jnp.int32))
    pair_output_update = pair_blocks.reshape(N, N, PAIR)
    grad_left = grad_lefts.transpose(1, 0, 2).reshape(SEQS, N, HID)
    grad_projected = jnp.concatenate([grad_left, grad_right.reshape(SEQS, N, HID)], axis=-1) * live[:, :, None]
    grad_low = grad_projected.astype(jnp.bfloat16)
    normalized_input_gradient = jnp.dot(grad_low.reshape(-1, 2 * HID), proj_weight.T, preferred_element_type=jnp.float32).reshape(SEQS, N, C)
    projection_weight_gradient = lax.dot_general(normed.reshape(-1, C), grad_low.reshape(-1, 2 * HID), (((0,), (0,)), ((), ())), preferred_element_type=jnp.float32)
    projection_bias_gradient = lax.optimization_barrier(jnp.sum(grad_projected, axis=(0, 1)))
    norm_gain_gradient = lax.optimization_barrier(jnp.sum(normalized_input_gradient * scaled_product, axis=(0, 1)))
    norm_shift_gradient = lax.optimization_barrier(jnp.sum(normalized_input_gradient, axis=(0, 1)))
    alignment_gradient = layer_norm_backward_pass(normalized_input_gradient, scaled_product, inverse_deviation, layer_norm_gain).astype(jnp.bfloat16)
    return (pair_output_update, alignment_gradient, norm_gain_gradient, norm_shift_gradient, projection_weight_gradient, projection_bias_gradient, output_weight_gradient)
```

```python
import functools

import jax
import jax.numpy as jnp
from jax import lax
from jax.experimental import pallas as pl
from jax.experimental.pallas import tpu as pltpu
from jax.sharding import PartitionSpec as P

EPSILON = 1e-05
LANES = 128
MESH = pl.DeviceIdType.MESH


def normalize(values, layer_norm_gain, norm_shift):
    widened = values.astype(jnp.float32)
    centred = widened - jnp.mean(widened, axis=-1, keepdims=True)
    inverse_deviation = lax.rsqrt(jnp.mean(centred * centred, axis=-1, keepdims=True) + EPSILON)
    scaled_product = centred * inverse_deviation
    return (
        scaled_product,
        inverse_deviation,
        (scaled_product * layer_norm_gain + norm_shift).astype(jnp.bfloat16),
    )


def layer_norm_backward_pass(
    normalized_input_gradient, scaled_product, inverse_deviation, layer_norm_gain
):
    grad_scaled = normalized_input_gradient * layer_norm_gain
    first = jnp.mean(grad_scaled, axis=-1, keepdims=True)
    second = jnp.mean(grad_scaled * scaled_product, axis=-1, keepdims=True)
    return inverse_deviation * (grad_scaled - first - scaled_product * second)


def route_gather_row(rows, cols):
    return dict(
        sends=rows,
        slots=rows,
        send=lambda t, r, c: (None, lax.rem(r + t, rows), c),
        mine=lambda r, c: r,
        source=lambda s, r, c: (s, c),
    )


def route_scatter_row(rows, cols):
    return dict(
        sends=rows,
        slots=rows,
        send=lambda t, r, c: (lax.rem(r + t, rows), lax.rem(r + t, rows), c),
        mine=lambda r, c: r,
        source=lambda s, r, c: (s, c),
    )


def route_tiles(rows, cols):
    factor = cols // rows
    return dict(
        sends=cols,
        slots=rows * factor,
        send=lambda t, r, c: (None, c // factor, lax.rem(c + t, cols)),
        mine=lambda r, c: r * factor + lax.rem(c, factor),
        source=lambda s, r, c: (s // factor, r * factor + lax.rem(s, factor)),
    )


def route_untile(rows, cols):
    factor = cols // rows

    def send(t, r, c):
        piece = lax.rem(r * factor + t, rows * factor)
        return piece, piece // factor, r * factor + lax.rem(piece, factor)

    return dict(
        sends=rows * factor,
        slots=cols,
        send=send,
        mine=lambda r, c: c,
        source=lambda s, r, c: (c // factor, s),
    )


def route_scatter_all(rows, cols):
    count = rows * cols

    def send(t, r, c):
        goal = lax.rem(r * cols + c + t, count)
        return goal, goal // cols, lax.rem(goal, cols)

    return dict(
        sends=count,
        slots=count,
        send=send,
        mine=lambda r, c: r * cols + c,
        source=lambda s, r, c: (s // cols, lax.rem(s, cols)),
    )


def route_gather_all(rows, cols):
    route = route_scatter_all(rows, cols)
    scatter_send = route["send"]
    route["send"] = lambda t, r, c: (None,) + scatter_send(t, r, c)[1:]
    return route


def exchange_kernel(routes, rows, cols, *refs):
    count = len(routes)
    sources, outs = refs[:count], refs[count : 2 * count]
    send_sems = refs[2 * count : 3 * count]
    recv_sems = refs[3 * count : 4 * count]
    local_sems = refs[4 * count]
    r = lax.axis_index("row")
    c = lax.axis_index("col")
    total = rows * cols
    barrier = pltpu.get_barrier_semaphore()

    def greet(t, carry):
        other = lax.rem(r * cols + c + t, total)
        pl.semaphore_signal(
            barrier,
            inc=1,
            device_id={"row": other // cols, "col": lax.rem(other, cols)},
            device_id_type=MESH,
        )
        return carry

    lax.fori_loop(1, total, greet, 0)
    pl.semaphore_wait(barrier, total - 1)

    def describe(k, t):
        piece, trow, tcol = routes[k]["send"](t, r, c)
        source = sources[k] if piece is None else sources[k].at[piece]
        slot = routes[k]["mine"](r, c)
        remote = pltpu.make_async_remote_copy(
            src_ref=source,
            dst_ref=outs[k].at[slot],
            send_sem=send_sems[k].at[t],
            recv_sem=recv_sems[k].at[slot],
            device_id={"row": trow, "col": tcol},
            device_id_type=MESH,
        )
        local = pltpu.make_async_copy(source, outs[k].at[slot], local_sems.at[k])
        here = jnp.logical_and(trow == r, tcol == c)
        return remote, local, here

    for k in range(count):

        def begin(t, carry, k=k):
            remote, local, here = describe(k, t)

            @pl.when(here)
            def _():
                local.start()
                local.wait()

            @pl.when(jnp.logical_not(here))
            def _():
                remote.start()

            return carry

        lax.fori_loop(0, routes[k]["sends"], begin, 0)

    for k in range(count):

        def finish(t, carry, k=k):
            remote, _, here = describe(k, t)

            @pl.when(jnp.logical_not(here))
            def _():
                remote.wait_send()

            return carry

        def receive(s, carry, k=k):
            srow, scol = routes[k]["source"](s, r, c)
            here = jnp.logical_and(srow == r, scol == c)
            arrival = pltpu.make_async_remote_copy(
                src_ref=outs[k].at[s],
                dst_ref=outs[k].at[s],
                send_sem=send_sems[k].at[0],
                recv_sem=recv_sems[k].at[s],
                device_id={"row": srow, "col": scol},
                device_id_type=MESH,
            )

            @pl.when(jnp.logical_not(here))
            def _():
                arrival.wait_recv()

            return carry

        lax.fori_loop(0, routes[k]["slots"], receive, 0)
        lax.fori_loop(0, routes[k]["sends"], finish, 0)


def exchange(arrays, makers, rows, cols, collective_id):
    routes = [maker(rows, cols) for maker in makers]
    shapes = []
    for array, route in zip(arrays, routes):
        block = array.shape if route["send"](0, 0, 0)[0] is None else array.shape[1:]
        shapes.append(jax.ShapeDtypeStruct((route["slots"],) + block, array.dtype))
    return pl.pallas_call(
        functools.partial(exchange_kernel, routes, rows, cols),
        out_shape=shapes,
        in_specs=[pl.BlockSpec(memory_space=pltpu.VMEM)] * len(arrays),
        out_specs=[pl.BlockSpec(memory_space=pltpu.VMEM)] * len(arrays),
        scratch_shapes=[pltpu.SemaphoreType.DMA((route["sends"],)) for route in routes]
        + [pltpu.SemaphoreType.DMA((route["slots"],)) for route in routes]
        + [pltpu.SemaphoreType.DMA((len(routes),))],
        compiler_params=pltpu.CompilerParams(collective_id=collective_id, has_side_effects=True),
    )(*arrays)


def pair_kernel(
    res,
    hidden,
    lt_ref,
    l_ref,
    r_ref,
    w_ref,
    cot_ref,
    div_ref,
    bias_ref,
    pair_ref,
    gw_ref,
    gl_ref,
    gr_ref,
    pre_ref,
    gpre_ref,
    glacc_ref,
):
    step = pl.program_id(0)
    fold = LANES // res
    seqs = r_ref.shape[0]
    major = l_ref.shape[0] // hidden

    @pl.when(step == 0)
    def _():
        gpre_ref[...] = (cot_ref[...].astype(jnp.float32) / div_ref[...]).astype(jnp.bfloat16)
        pre_ref[...] = jnp.zeros_like(pre_ref)
        glacc_ref[...] = jnp.zeros_like(glacc_ref)

    group = lax.broadcasted_iota(jnp.int32, (seqs, LANES), 1) // res
    wide = jnp.concatenate([group] * fold, axis=1)

    def spread(x):
        out = x
        for k in range(1, fold):
            out = out + pltpu.roll(x, k * res, 1)
        return out

    chunk = r_ref[...].astype(jnp.float32)
    copies = jnp.concatenate(
        [spread(jnp.where(group == d, chunk, 0.0)) for d in range(fold)], axis=1
    )
    masked = jnp.concatenate(
        [jnp.where(wide == i, copies, 0.0).astype(jnp.bfloat16) for i in range(fold)], axis=0
    )
    tile = jnp.dot(l_ref[...], masked, preferred_element_type=jnp.float32).astype(jnp.bfloat16)
    products = jnp.concatenate(
        [
            jnp.concatenate(
                [
                    tile[i * hidden : (i + 1) * hidden, d * LANES : (d + 1) * LANES]
                    for i in range(major)
                ],
                axis=1,
            )
            for d in range(fold)
        ],
        axis=0,
    )
    weight = w_ref[...]
    grad_pre = gpre_ref[...]
    pre_ref[...] += lax.dot_general(
        products, weight, (((0,), (0,)), ((), ())), preferred_element_type=jnp.float32
    )
    gw_ref[...] = jnp.dot(products, grad_pre, preferred_element_type=jnp.float32).astype(
        gw_ref.dtype
    )
    grad_products = lax.dot_general(
        weight, grad_pre, (((1,), (1,)), ((), ())), preferred_element_type=jnp.float32
    ).astype(jnp.bfloat16)
    grad_tile = jnp.concatenate(
        [
            jnp.concatenate(
                [
                    grad_products[d * hidden : (d + 1) * hidden, i * LANES : (i + 1) * LANES]
                    for d in range(fold)
                ],
                axis=1,
            )
            for i in range(major)
        ],
        axis=0,
    )
    glacc_ref[...] += lax.dot_general(
        masked, grad_tile, (((1,), (1,)), ((), ())), preferred_element_type=jnp.float32
    )
    grad_right = jnp.zeros((seqs, fold * LANES), jnp.float32)
    for i in range(fold):
        part = jnp.dot(
            lt_ref[i * seqs : (i + 1) * seqs, :], grad_tile, preferred_element_type=jnp.float32
        )
        grad_right = jnp.where(wide == i, part, grad_right)
    packed = jnp.zeros((seqs, LANES), jnp.float32)
    for d in range(fold):
        packed = jnp.where(
            group == d, spread(grad_right[:, d * LANES : (d + 1) * LANES]), packed
        )
    gr_ref[...] = packed.astype(gr_ref.dtype)

    @pl.when(step == pl.num_programs(0) - 1)
    def _():
        pair_ref[...] = ((pre_ref[...] + bias_ref[...]) / div_ref[...]).astype(pair_ref.dtype)
        gl_ref[...] = glacc_ref[...].astype(gl_ref.dtype)


def pair_tile(lt, right, weight, cotangent, divisor, bias, res, hidden):
    fold = LANES // res
    pairs, width = cotangent.shape
    seqs = right.shape[0]
    rows = lt.shape[1]

    def whole(shape):
        return pl.BlockSpec(shape, lambda k: (0,) * len(shape))

    return pl.pallas_call(
        functools.partial(pair_kernel, res, hidden),
        grid=(hidden // fold,),
        in_specs=[
            whole(lt.shape),
            whole(lt.shape[::-1]),
            pl.BlockSpec((seqs, LANES), lambda k: (0, k)),
            pl.BlockSpec((fold * hidden, width), lambda k: (k, 0)),
            whole((pairs, width)),
            whole((pairs, 1)),
            whole((1, width)),
        ],
        out_specs=[
            whole((pairs, width)),
            pl.BlockSpec((fold * hidden, width), lambda k: (k, 0)),
            whole(lt.shape),
            pl.BlockSpec((seqs, LANES), lambda k: (0, k)),
        ],
        out_shape=[
            jax.ShapeDtypeStruct((pairs, width), jnp.bfloat16),
            jax.ShapeDtypeStruct((hidden * hidden, width), jnp.bfloat16),
            jax.ShapeDtypeStruct(lt.shape, jnp.bfloat16),
            jax.ShapeDtypeStruct((seqs, hidden * res), jnp.bfloat16),
        ],
        scratch_shapes=[
            pltpu.VMEM((pairs, width), jnp.float32),
            pltpu.VMEM((pairs, width), jnp.bfloat16),
            pltpu.VMEM((fold * seqs, rows), jnp.float32),
        ],
        compiler_params=pltpu.CompilerParams(dimension_semantics=("arbitrary",)),
    )(lt, lt.T, right, weight, cotangent, divisor, bias)


def shards(
    alignment,
    sequence_mask,
    residue_mask,
    layer_norm_gain,
    norm_shift,
    proj_weight,
    proj_bias,
    out_weight,
    out_bias,
    cotangent,
):
    rows = lax.axis_size("row")
    cols = lax.axis_size("col")
    total = rows * cols
    factor = cols // rows
    row_index = lax.axis_index("row")
    col_index = lax.axis_index("col")
    seq_local, res_local, channels = alignment.shape
    seqs = seq_local * rows
    hidden = proj_weight.shape[1] // 2
    pair_width = out_weight.shape[1]
    tile_rows = res_local * factor
    fold = LANES // res_local
    inner = res_local // fold
    scaled_product, inverse_deviation, normed = normalize(alignment, layer_norm_gain, norm_shift)
    seq_here = lax.dynamic_slice_in_dim(sequence_mask, row_index * seq_local, seq_local)
    res_here = lax.dynamic_slice_in_dim(residue_mask, col_index * res_local, res_local)
    live = (seq_here[:, None] * res_here[None, :]).astype(jnp.float32)
    projected = jnp.dot(
        normed.reshape(-1, channels), proj_weight, preferred_element_type=jnp.float32
    )
    projected = projected.reshape(seq_local, res_local, 2 * hidden) + proj_bias
    masked = (projected * live[:, :, None]).astype(jnp.bfloat16)
    left_send = (
        masked[:, :, :hidden]
        .reshape(seq_local, inner, fold, hidden)
        .transpose(2, 0, 1, 3)
        .reshape(fold, seq_local, inner * hidden)
    )
    right_send = masked[:, :, hidden:].transpose(0, 2, 1).reshape(seq_local, hidden * res_local)
    lefts, rights = exchange(
        [left_send, right_send], [route_tiles, route_gather_row], rows, cols, 0
    )
    lt = (
        lefts.reshape(rows, factor, fold, seq_local, inner * hidden)
        .transpose(2, 0, 3, 1, 4)
        .reshape(fold * seqs, factor * inner * hidden)
    )
    right = rights.reshape(seqs, hidden * res_local)
    kept_count = jnp.sum(sequence_mask).astype(jnp.float32)
    tile_live = lax.dynamic_slice_in_dim(residue_mask, row_index * tile_rows, tile_rows).astype(
        jnp.float32
    )
    column_live = res_here.astype(jnp.float32)
    divisor = jnp.maximum(kept_count * tile_live[:, None] * column_live[None, :], 1.0).reshape(
        -1, 1
    )
    swapped = (
        out_weight.reshape(hidden, hidden, pair_width)
        .transpose(1, 0, 2)
        .reshape(hidden * hidden, pair_width)
    )
    pair, grad_w, grad_lt, grad_r = pair_tile(
        lt,
        right,
        swapped,
        cotangent.reshape(-1, pair_width),
        divisor,
        out_bias.reshape(1, -1),
        res_local,
        hidden,
    )
    pair_output_update = pair.reshape(tile_rows, res_local, pair_width)
    left_parts = (
        grad_lt.reshape(fold, rows, seq_local, factor, inner * hidden)
        .transpose(1, 3, 0, 2, 4)
        .reshape(rows * factor, fold, seq_local, inner * hidden)
    )
    got_left, got_right, got_w = exchange(
        [
            left_parts,
            grad_r.reshape(rows, seq_local, hidden * res_local),
            grad_w.reshape(total, -1, pair_width),
        ],
        [route_untile, route_scatter_row, route_scatter_all],
        rows,
        cols,
        1,
    )
    grad_left = (
        jnp.sum(got_left.astype(jnp.float32), axis=0)
        .reshape(fold, seq_local, inner, hidden)
        .transpose(1, 2, 0, 3)
        .reshape(seq_local, res_local, hidden)
    )
    grad_right = (
        jnp.sum(got_right.astype(jnp.float32), axis=0)
        .reshape(seq_local, hidden, res_local)
        .transpose(0, 2, 1)
    )
    grad_w_here = jnp.sum(got_w.astype(jnp.float32), axis=0).astype(jnp.bfloat16)
    grad_projected = jnp.concatenate([grad_left, grad_right], axis=-1) * live[:, :, None]
    grad_low = grad_projected.astype(jnp.bfloat16)
    normalized_input_gradient = jnp.dot(
        grad_low.reshape(-1, 2 * hidden), proj_weight.T, preferred_element_type=jnp.float32
    ).reshape(seq_local, res_local, channels)
    weight_local = lax.dot_general(
        normed.reshape(-1, channels),
        grad_low.reshape(-1, 2 * hidden),
        (((0,), (0,)), ((), ())),
        preferred_element_type=jnp.float32,
    )
    bias_local = jnp.sum(grad_projected, axis=(0, 1))
    gain_local = jnp.sum(normalized_input_gradient * scaled_product, axis=(0, 1))
    shift_local = jnp.sum(normalized_input_gradient, axis=(0, 1))
    alignment_gradient = layer_norm_backward_pass(
        normalized_input_gradient, scaled_product, inverse_deviation, layer_norm_gain
    ).astype(jnp.bfloat16)
    vectors = jnp.stack(
        [gain_local, shift_local, jnp.pad(bias_local, (0, channels - 2 * hidden))]
    )
    all_w, all_weight, all_vectors = exchange(
        [grad_w_here, weight_local.T.astype(jnp.bfloat16), vectors],
        [route_gather_all] * 3,
        rows,
        cols,
        2,
    )
    output_weight_gradient = (
        all_w.reshape(hidden, hidden, pair_width)
        .transpose(1, 0, 2)
        .reshape(hidden * hidden, pair_width)
        .astype(jnp.float32)
    )
    weight_sum = jnp.sum(all_weight.astype(jnp.float32), axis=0).T
    vector_sum = jnp.sum(all_vectors, axis=0)
    return (
        pair_output_update,
        alignment_gradient,
        vector_sum[0],
        vector_sum[1],
        weight_sum,
        vector_sum[2, : 2 * hidden],
        output_weight_gradient,
    )


def solution(mesh):
    return jax.shard_map(
        shards,
        mesh=mesh,
        in_specs=(
            P(("groups", "row"), "col", None),
            P("groups"),
            P("groups"),
            P(),
            P(),
            P(),
            P(),
            P(),
            P(),
            P(("groups", "row"), "col", None),
        ),
        out_specs=(
            P(("groups", "row"), "col", None),
            P(("groups", "row"), "col", None),
            P("groups"),
            P("groups"),
            P("groups", None),
            P("groups"),
            P("groups", None),
        ),
        check_vma=False,
    )
```

```python
import functools

import jax
import jax.numpy as jnp
from jax import lax
from jax.experimental import pallas as pl
from jax.experimental.pallas import tpu as pltpu
from jax.sharding import PartitionSpec as P

EPSILON = 1e-05
LANES = 128
MESH = pl.DeviceIdType.MESH


def normalize(values, layer_norm_gain, norm_shift):
    widened = values.astype(jnp.float32)
    centred = widened - jnp.mean(widened, axis=-1, keepdims=True)
    inverse_deviation = lax.rsqrt(jnp.mean(centred * centred, axis=-1, keepdims=True) + EPSILON)
    scaled_product = centred * inverse_deviation
    return (
        scaled_product,
        inverse_deviation,
        (scaled_product * layer_norm_gain + norm_shift).astype(jnp.bfloat16),
    )


def layer_norm_backward_pass(
    normalized_input_gradient, scaled_product, inverse_deviation, layer_norm_gain
):
    grad_scaled = normalized_input_gradient * layer_norm_gain
    first = jnp.mean(grad_scaled, axis=-1, keepdims=True)
    second = jnp.mean(grad_scaled * scaled_product, axis=-1, keepdims=True)
    return inverse_deviation * (grad_scaled - first - scaled_product * second)


def route_gather_row(rows, cols):
    return dict(
        sends=rows,
        slots=rows,
        send=lambda t, r, c: (None, lax.rem(r + t, rows), c),
        mine=lambda r, c: r,
        source=lambda s, r, c: (s, c),
    )


def route_scatter_row(rows, cols):
    return dict(
        sends=rows,
        slots=rows,
        send=lambda t, r, c: (lax.rem(r + t, rows), lax.rem(r + t, rows), c),
        mine=lambda r, c: r,
        source=lambda s, r, c: (s, c),
    )


def route_gather_col(rows, cols):
    return dict(
        sends=cols,
        slots=cols,
        send=lambda t, r, c: (None, r, lax.rem(c + t, cols)),
        mine=lambda r, c: c,
        source=lambda s, r, c: (r, s),
    )


def route_scatter_col(rows, cols):
    return dict(
        sends=cols,
        slots=cols,
        send=lambda t, r, c: (lax.rem(c + t, cols), r, lax.rem(c + t, cols)),
        mine=lambda r, c: c,
        source=lambda s, r, c: (r, s),
    )


def route_tiles(rows, cols):
    factor = cols // rows
    return dict(
        sends=cols,
        slots=rows * factor,
        send=lambda t, r, c: (None, c // factor, lax.rem(c + t, cols)),
        mine=lambda r, c: r * factor + lax.rem(c, factor),
        source=lambda s, r, c: (s // factor, r * factor + lax.rem(s, factor)),
    )


def route_untile(rows, cols):
    factor = cols // rows

    def send(t, r, c):
        piece = lax.rem(r * factor + t, rows * factor)
        return piece, piece // factor, r * factor + lax.rem(piece, factor)

    return dict(
        sends=rows * factor,
        slots=cols,
        send=send,
        mine=lambda r, c: c,
        source=lambda s, r, c: (c // factor, s),
    )


def route_scatter_all(rows, cols):
    count = rows * cols

    def send(t, r, c):
        goal = lax.rem(r * cols + c + t, count)
        return goal, goal // cols, lax.rem(goal, cols)

    return dict(
        sends=count,
        slots=count,
        send=send,
        mine=lambda r, c: r * cols + c,
        source=lambda s, r, c: (s // cols, lax.rem(s, cols)),
    )


def route_gather_all(rows, cols):
    route = route_scatter_all(rows, cols)
    scatter_send = route["send"]
    route["send"] = lambda t, r, c: (None,) + scatter_send(t, r, c)[1:]
    return route


def exchange_kernel(routes, rows, cols, along_row, *refs):
    count = len(routes)
    sources, outs = refs[:count], refs[count : 2 * count]
    send_sems = refs[2 * count : 3 * count]
    recv_sems = refs[3 * count : 4 * count]
    local_sems = refs[4 * count]
    r = lax.axis_index("row")
    c = lax.axis_index("col")
    total = rows if along_row else rows * cols
    barrier = pltpu.get_barrier_semaphore()

    def greet(t, carry):
        if along_row:
            orow, ocol = lax.rem(r + t, total), c
        else:
            other = lax.rem(r * cols + c + t, total)
            orow, ocol = other // cols, lax.rem(other, cols)
        pl.semaphore_signal(
            barrier,
            inc=1,
            device_id={"row": orow, "col": ocol},
            device_id_type=MESH,
        )
        return carry

    lax.fori_loop(1, total, greet, 0)
    pl.semaphore_wait(barrier, total - 1)

    def describe(k, t):
        piece, trow, tcol = routes[k]["send"](t, r, c)
        source = sources[k] if piece is None else sources[k].at[piece]
        slot = routes[k]["mine"](r, c)
        remote = pltpu.make_async_remote_copy(
            src_ref=source,
            dst_ref=outs[k].at[slot],
            send_sem=send_sems[k].at[t],
            recv_sem=recv_sems[k].at[slot],
            device_id={"row": trow, "col": tcol},
            device_id_type=MESH,
        )
        here = jnp.logical_and(trow == r, tcol == c)
        return remote, source, outs[k].at[slot], here

    for k in range(count):

        def begin(t, carry, k=k):
            remote, source, target, here = describe(k, t)

            @pl.when(here)
            def _():
                local = pltpu.make_async_copy(source, target, local_sems.at[k])
                local.start()
                local.wait()

            @pl.when(jnp.logical_not(here))
            def _():
                remote.start()

            return carry

        lax.fori_loop(0, routes[k]["sends"], begin, 0)

    for k in range(count):

        def finish(t, carry, k=k):
            remote, _, _, here = describe(k, t)

            @pl.when(jnp.logical_not(here))
            def _():
                remote.wait_send()

            return carry

        def receive(s, carry, k=k):
            srow, scol = routes[k]["source"](s, r, c)
            here = jnp.logical_and(srow == r, scol == c)
            arrival = pltpu.make_async_remote_copy(
                src_ref=outs[k].at[s],
                dst_ref=outs[k].at[s],
                send_sem=send_sems[k].at[0],
                recv_sem=recv_sems[k].at[s],
                device_id={"row": srow, "col": scol},
                device_id_type=MESH,
            )

            @pl.when(jnp.logical_not(here))
            def _():
                arrival.wait_recv()

            return carry

        lax.fori_loop(0, routes[k]["slots"], receive, 0)
        lax.fori_loop(0, routes[k]["sends"], finish, 0)


def exchange(arrays, makers, rows, cols, collective_id, along_row=False):
    routes = [maker(rows, cols) for maker in makers]
    shapes = []
    for array, route in zip(arrays, routes):
        block = array.shape if route["send"](0, 0, 0)[0] is None else array.shape[1:]
        shapes.append(jax.ShapeDtypeStruct((route["slots"],) + block, array.dtype))
    return pl.pallas_call(
        functools.partial(exchange_kernel, routes, rows, cols, along_row),
        out_shape=shapes,
        in_specs=[pl.BlockSpec(memory_space=pltpu.VMEM)] * len(arrays),
        out_specs=[pl.BlockSpec(memory_space=pltpu.VMEM)] * len(arrays),
        scratch_shapes=[pltpu.SemaphoreType.DMA((route["sends"],)) for route in routes]
        + [pltpu.SemaphoreType.DMA((route["slots"],)) for route in routes]
        + [pltpu.SemaphoreType.DMA((len(routes),))],
        compiler_params=pltpu.CompilerParams(collective_id=collective_id, has_side_effects=True),
    )(*arrays)


def pair_kernel(
    res,
    hidden,
    lt_ref,
    l_ref,
    r_ref,
    w_ref,
    cot_ref,
    div_ref,
    bias_ref,
    pair_ref,
    gw_ref,
    gl_ref,
    gr_ref,
    pre_ref,
    gpre_ref,
    glacc_ref,
):
    step = pl.program_id(0)
    fold = LANES // res
    seqs = r_ref.shape[0]
    major = l_ref.shape[0] // hidden

    @pl.when(step == 0)
    def _():
        gpre_ref[...] = (cot_ref[...].astype(jnp.float32) / div_ref[...]).astype(jnp.bfloat16)
        pre_ref[...] = jnp.zeros_like(pre_ref)
        glacc_ref[...] = jnp.zeros_like(glacc_ref)

    group = lax.broadcasted_iota(jnp.int32, (seqs, LANES), 1) // res
    wide = jnp.concatenate([group] * fold, axis=1)

    def spread(x):
        out = x
        for k in range(1, fold):
            out = out + pltpu.roll(x, k * res, 1)
        return out

    chunk = r_ref[...].astype(jnp.float32)
    copies = jnp.concatenate(
        [spread(jnp.where(group == d, chunk, 0.0)) for d in range(fold)], axis=1
    )
    masked = jnp.concatenate(
        [jnp.where(wide == i, copies, 0.0).astype(jnp.bfloat16) for i in range(fold)], axis=0
    )
    tile = jnp.dot(l_ref[...], masked, preferred_element_type=jnp.float32).astype(jnp.bfloat16)
    products = jnp.concatenate(
        [
            jnp.concatenate(
                [
                    tile[i * hidden : (i + 1) * hidden, d * LANES : (d + 1) * LANES]
                    for i in range(major)
                ],
                axis=1,
            )
            for d in range(fold)
        ],
        axis=0,
    )
    weight = w_ref[...]
    grad_pre = gpre_ref[...]
    pre_ref[...] += lax.dot_general(
        products, weight, (((0,), (0,)), ((), ())), preferred_element_type=jnp.float32
    )
    gw_ref[...] = jnp.dot(products, grad_pre, preferred_element_type=jnp.float32).astype(
        gw_ref.dtype
    )
    grad_products = lax.dot_general(
        weight, grad_pre, (((1,), (1,)), ((), ())), preferred_element_type=jnp.float32
    ).astype(jnp.bfloat16)
    grad_tile = jnp.concatenate(
        [
            jnp.concatenate(
                [
                    grad_products[d * hidden : (d + 1) * hidden, i * LANES : (i + 1) * LANES]
                    for d in range(fold)
                ],
                axis=1,
            )
            for i in range(major)
        ],
        axis=0,
    )
    glacc_ref[...] += lax.dot_general(
        masked, grad_tile, (((1,), (1,)), ((), ())), preferred_element_type=jnp.float32
    )
    grad_right = jnp.zeros((seqs, fold * LANES), jnp.float32)
    for i in range(fold):
        part = jnp.dot(
            lt_ref[i * seqs : (i + 1) * seqs, :], grad_tile, preferred_element_type=jnp.float32
        )
        grad_right = jnp.where(wide == i, part, grad_right)
    packed = jnp.zeros((seqs, LANES), jnp.float32)
    for d in range(fold):
        packed = jnp.where(
            group == d, spread(grad_right[:, d * LANES : (d + 1) * LANES]), packed
        )
    gr_ref[...] = packed.astype(gr_ref.dtype)

    @pl.when(step == pl.num_programs(0) - 1)
    def _():
        pair_ref[...] = ((pre_ref[...] + bias_ref[...]) / div_ref[...]).astype(pair_ref.dtype)
        gl_ref[...] = glacc_ref[...].astype(gl_ref.dtype)


def pair_tile(lt, right, weight, cotangent, divisor, bias, res, hidden):
    fold = LANES // res
    pairs, width = cotangent.shape
    seqs = right.shape[0]
    rows = lt.shape[1]

    def whole(shape):
        return pl.BlockSpec(shape, lambda k: (0,) * len(shape))

    return pl.pallas_call(
        functools.partial(pair_kernel, res, hidden),
        grid=(hidden // fold,),
        in_specs=[
            whole(lt.shape),
            whole(lt.shape[::-1]),
            pl.BlockSpec((seqs, LANES), lambda k: (0, k)),
            pl.BlockSpec((fold * hidden, width), lambda k: (k, 0)),
            whole((pairs, width)),
            whole((pairs, 1)),
            whole((1, width)),
        ],
        out_specs=[
            whole((pairs, width)),
            pl.BlockSpec((fold * hidden, width), lambda k: (k, 0)),
            whole(lt.shape),
            pl.BlockSpec((seqs, LANES), lambda k: (0, k)),
        ],
        out_shape=[
            jax.ShapeDtypeStruct((pairs, width), jnp.bfloat16),
            jax.ShapeDtypeStruct((hidden * hidden, width), jnp.bfloat16),
            jax.ShapeDtypeStruct(lt.shape, jnp.bfloat16),
            jax.ShapeDtypeStruct((seqs, hidden * res), jnp.bfloat16),
        ],
        scratch_shapes=[
            pltpu.VMEM((pairs, width), jnp.float32),
            pltpu.VMEM((pairs, width), jnp.bfloat16),
            pltpu.VMEM((fold * seqs, rows), jnp.float32),
        ],
        compiler_params=pltpu.CompilerParams(dimension_semantics=("arbitrary",)),
    )(lt, lt.T, right, weight, cotangent, divisor, bias)


def shards(
    alignment,
    sequence_mask,
    residue_mask,
    layer_norm_gain,
    norm_shift,
    proj_weight,
    proj_bias,
    out_weight,
    out_bias,
    cotangent,
):
    rows = lax.axis_size("row")
    cols = lax.axis_size("col")
    factor = cols // rows
    row_index = lax.axis_index("row")
    col_index = lax.axis_index("col")
    seq_local, res_local, channels = alignment.shape
    seqs = seq_local * rows
    hidden = proj_weight.shape[1] // 2
    pair_width = out_weight.shape[1]
    tile_rows = res_local * factor
    fold = LANES // res_local
    inner = res_local // fold
    scaled_product, inverse_deviation, normed = normalize(alignment, layer_norm_gain, norm_shift)
    seq_here = lax.dynamic_slice_in_dim(sequence_mask, row_index * seq_local, seq_local)
    res_here = lax.dynamic_slice_in_dim(residue_mask, col_index * res_local, res_local)
    live = (seq_here[:, None] * res_here[None, :]).astype(jnp.float32)
    projected = jnp.dot(
        normed.reshape(-1, channels), proj_weight, preferred_element_type=jnp.float32
    )
    projected = projected.reshape(seq_local, res_local, 2 * hidden) + proj_bias
    masked = (projected * live[:, :, None]).astype(jnp.bfloat16)
    left_send = (
        masked[:, :, :hidden]
        .reshape(seq_local, inner, fold, hidden)
        .transpose(2, 0, 1, 3)
        .reshape(fold, seq_local, inner * hidden)
    )
    right_send = masked[:, :, hidden:].transpose(0, 2, 1).reshape(seq_local, hidden * res_local)
    lefts, rights = exchange(
        [left_send, right_send], [route_tiles, route_gather_row], rows, cols, 0
    )
    lt = (
        lefts.reshape(rows, factor, fold, seq_local, inner * hidden)
        .transpose(2, 0, 3, 1, 4)
        .reshape(fold * seqs, factor * inner * hidden)
    )
    right = rights.reshape(seqs, hidden * res_local)
    kept_count = jnp.sum(sequence_mask).astype(jnp.float32)
    tile_live = lax.dynamic_slice_in_dim(residue_mask, row_index * tile_rows, tile_rows).astype(
        jnp.float32
    )
    column_live = res_here.astype(jnp.float32)
    divisor = jnp.maximum(kept_count * tile_live[:, None] * column_live[None, :], 1.0).reshape(
        -1, 1
    )
    swapped = (
        out_weight.reshape(hidden, hidden, pair_width)
        .transpose(1, 0, 2)
        .reshape(hidden * hidden, pair_width)
    )
    pair, grad_w, grad_lt, grad_r = pair_tile(
        lt,
        right,
        swapped,
        cotangent.reshape(-1, pair_width),
        divisor,
        out_bias.reshape(1, -1),
        res_local,
        hidden,
    )
    pair_output_update = pair.reshape(tile_rows, res_local, pair_width)
    left_parts = (
        grad_lt.reshape(fold, rows, seq_local, factor, inner * hidden)
        .transpose(1, 3, 0, 2, 4)
        .reshape(rows * factor, fold, seq_local, inner * hidden)
    )
    got_left, got_right, got_w = exchange(
        [
            left_parts,
            grad_r.reshape(rows, seq_local, hidden * res_local),
            grad_w.reshape(cols, -1, pair_width),
        ],
        [route_untile, route_scatter_row, route_scatter_col],
        rows,
        cols,
        1,
    )
    grad_left = (
        jnp.sum(got_left.astype(jnp.float32), axis=0)
        .reshape(fold, seq_local, inner, hidden)
        .transpose(1, 2, 0, 3)
        .reshape(seq_local, res_local, hidden)
    )
    grad_right = (
        jnp.sum(got_right.astype(jnp.float32), axis=0)
        .reshape(seq_local, hidden, res_local)
        .transpose(0, 2, 1)
    )
    grad_w_col = jnp.sum(got_w.astype(jnp.float32), axis=0).astype(jnp.bfloat16)
    grad_projected = jnp.concatenate([grad_left, grad_right], axis=-1) * live[:, :, None]
    grad_low = grad_projected.astype(jnp.bfloat16)
    normalized_input_gradient = jnp.dot(
        grad_low.reshape(-1, 2 * hidden), proj_weight.T, preferred_element_type=jnp.float32
    ).reshape(seq_local, res_local, channels)
    weight_local = lax.dot_general(
        normed.reshape(-1, channels),
        grad_low.reshape(-1, 2 * hidden),
        (((0,), (0,)), ((), ())),
        preferred_element_type=jnp.float32,
    )
    bias_local = jnp.sum(grad_projected, axis=(0, 1))
    gain_local = jnp.sum(normalized_input_gradient * scaled_product, axis=(0, 1))
    shift_local = jnp.sum(normalized_input_gradient, axis=(0, 1))
    alignment_gradient = layer_norm_backward_pass(
        normalized_input_gradient, scaled_product, inverse_deviation, layer_norm_gain
    ).astype(jnp.bfloat16)
    vectors = jnp.stack(
        [gain_local, shift_local, jnp.pad(bias_local, (0, channels - 2 * hidden))]
    )
    row_w, row_weight, row_vectors = exchange(
        [
            grad_w_col.reshape(rows, -1, pair_width),
            weight_local.T.astype(jnp.bfloat16),
            vectors,
        ],
        [route_scatter_row, route_gather_row, route_gather_row],
        rows,
        cols,
        2,
        along_row=True,
    )
    all_w, all_weight, all_vectors = exchange(
        [
            jnp.sum(row_w.astype(jnp.float32), axis=0).astype(jnp.bfloat16),
            jnp.sum(row_weight.astype(jnp.float32), axis=0).astype(jnp.bfloat16),
            jnp.sum(row_vectors, axis=0),
        ],
        [route_gather_all, route_gather_col, route_gather_col],
        rows,
        cols,
        3,
    )
    output_weight_gradient = (
        all_w.reshape(rows, cols, -1, pair_width)
        .transpose(1, 0, 2, 3)
        .reshape(hidden, hidden, pair_width)
        .transpose(1, 0, 2)
        .reshape(hidden * hidden, pair_width)
        .astype(jnp.float32)
    )
    weight_sum = jnp.sum(all_weight.astype(jnp.float32), axis=0).T
    vector_sum = jnp.sum(all_vectors, axis=0)
    return (
        pair_output_update,
        alignment_gradient,
        vector_sum[0],
        vector_sum[1],
        weight_sum,
        vector_sum[2, : 2 * hidden],
        output_weight_gradient,
    )


def solution(mesh):
    return jax.shard_map(
        shards,
        mesh=mesh,
        in_specs=(
            P(("groups", "row"), "col", None),
            P("groups"),
            P("groups"),
            P(),
            P(),
            P(),
            P(),
            P(),
            P(),
            P(("groups", "row"), "col", None),
        ),
        out_specs=(
            P(("groups", "row"), "col", None),
            P(("groups", "row"), "col", None),
            P("groups"),
            P("groups"),
            P("groups", None),
            P("groups"),
            P("groups", None),
        ),
        check_vma=False,
    )
```
